512 devices in a mesh: blk: 32 (over y, x), harm: 16 (over z, core).
Axes of the slice: x: 4, y: 8, z: 8, core: 2. Of those that a mesh axis runs over, the one named last changes fastest.
Arguments:
- samples: float32 [16384, 128], P(('blk', 'harm')), may hold values from -6 to 6
- store: float32 [2, 48, 16384, 128], P(None, 'harm', 'blk'), may hold values from -0.6 to 0.6
- phase: float32 [5], replicated, may hold values from -3.140625 to 3.140625
- patch_row: int32 [16384], P('blk'), may hold values from 0 to 4
- harm_counts: int32 [5], replicated, may hold values from 8 to 48
- freq_index: int32 [5, 48], replicated, may hold values from 1 to 63
- blade_counts: int32 [5], replicated, may hold values from 20 to 80
Outputs:
- new_store: float32 [2, 48, 16384, 128], P(None, 'harm', 'blk')
- lower_lagged: float32 [16384, 128], P(('blk', 'harm'))
- upper_lagged: float32 [16384, 128], P(('blk', 'harm'))
The draws below stay inside these ranges and needn't reach their ends.
All inputs are finite; a program needn't handle non-finite values.
Results may differ from the reference program's by a relative error of at most 0.00002.
Values sent between devices are 32-bit elements; how exact they have to be, the bound alone decides.
A program may use at most 64 MiB of HBM per device.

```python
import jax
import jax.numpy as jnp
from jax import lax

ROWS = 5
KMAX = 48
POINTS = 128
PATCHES = 16384
N_BLK = 32


def plant(values, own_key, smallest, largest):
    extent = values.shape
    index_at = [jax.random.randint(jax.random.fold_in(own_key, axis), (), 0, extent[axis]) for axis in range(len(extent))]
    values = values.at[tuple(index_at)].set(smallest)
    longest = extent.index(max(extent))
    index_at[longest] = (index_at[longest] + 1) % extent[longest]
    return values.at[tuple(index_at)].set(largest)


def steps_of(stream_key, extent, cuts, smallest, largest):
    def one(axis_at, blocks):
        heights = jax.random.uniform(jax.random.fold_in(jax.random.fold_in(stream_key, 6), axis_at), (blocks,), jnp.float32, smallest / len(cuts), largest / len(cuts))
        return jnp.repeat(jnp.exp(heights), extent[axis_at] // blocks).reshape((-1,) + (1,) * (len(extent) - axis_at - 1))

    level = one(*cuts[0])
    for cut in cuts[1:]:
        level = level * one(*cut)
    return level


def normal_values(key, extent, deviation, most, pieces=(), kind=jnp.bfloat16):
    entries = jax.random.normal(key, extent, jnp.float32) * deviation
    if len(pieces) > 0:
        entries = steps_of(key, extent, pieces, -0.22, 0.18) * entries
    return jnp.clip(entries, min=-most, max=most).astype(kind)


def setup_inputs(seed: int = 0) -> dict:
    seeds = jax.random.split(jax.random.key(seed), 8)
    samples = normal_values(seeds[0], (PATCHES, POINTS), 1.0, 6.0, ((0, 512),), jnp.float32)
    store = normal_values(seeds[1], (2, KMAX, PATCHES, POINTS), 0.1, 0.6, ((1, 16), (2, 32)), jnp.float32)
    phase = jnp.clip(jax.random.uniform(seeds[2], (ROWS,), jnp.float32, -3.140625, 3.140625), -3.140625, 3.140625)
    patch_row = plant(jax.random.randint(seeds[3], (PATCHES,), 0, 5), jax.random.fold_in(seeds[3], 1), 0, 4).astype(jnp.int32)
    harm_counts = plant(jax.random.randint(seeds[4], (ROWS,), 8, 49), jax.random.fold_in(seeds[4], 1), 8, 48).astype(jnp.int32)
    freq_index = plant(jax.random.randint(seeds[5], (ROWS, KMAX), 1, 64), jax.random.fold_in(seeds[5], 1), 1, 63).astype(jnp.int32)
    blade_counts = plant(jax.random.randint(seeds[6], (ROWS,), 20, 81), jax.random.fold_in(seeds[6], 1), 20, 80).astype(jnp.int32)
    return {"samples": samples, "store": store, "phase": phase, "patch_row": patch_row, "harm_counts": harm_counts, "freq_index": freq_index, "blade_counts": blade_counts}


relax_rate = 0.3


def reference(samples, store, phase, patch_row, harm_counts, freq_index, blade_counts):
    frequency = freq_index.astype(jnp.float32)
    angle_row = frequency * phase[:, None]
    lag_row = 2.0 * jnp.pi * frequency / blade_counts.astype(jnp.float32)[:, None]
    slot_ids = jnp.arange(KMAX, dtype=jnp.int32)
    active_row = slot_ids[None, :] < harm_counts[:, None]
    angle_now = angle_row[patch_row].T
    angle_lag = lag_row[patch_row].T
    active_mask = active_row[patch_row].T

    def step(carry, items):
        back_sum, ahead_sum = carry
        cos_old, sin_old, now_col, lag_col, mask_col = items
        now_c = jnp.cos(now_col)[:, None]
        now_s = jnp.sin(now_col)[:, None]
        mask_b = mask_col[:, None]
        cos_new = jnp.where(mask_b, cos_old + relax_rate * (2.0 * samples * now_c - cos_old), cos_old)
        sin_new = jnp.where(mask_b, sin_old + relax_rate * (2.0 * samples * now_s - sin_old), sin_old)
        back_angle = (now_col - lag_col)[:, None]
        ahead_angle = (now_col + lag_col)[:, None]
        back_term = cos_new * jnp.cos(back_angle) + sin_new * jnp.sin(back_angle)
        ahead_term = cos_new * jnp.cos(ahead_angle) + sin_new * jnp.sin(ahead_angle)
        back_sum = back_sum + jnp.where(mask_b, back_term, 0.0)
        ahead_sum = ahead_sum + jnp.where(mask_b, ahead_term, 0.0)
        return (back_sum, ahead_sum), (cos_new, sin_new)

    zeros_field = jnp.zeros(samples.shape, jnp.float32)
    (back_sum, ahead_sum), (cos_all, sin_all) = lax.scan(step, (zeros_field, zeros_field), (store[0], store[1], angle_now, angle_lag, active_mask))
    new_store = jnp.stack([cos_all, sin_all])
    block_size = PATCHES // N_BLK
    lower_lagged = jnp.roll(back_sum, block_size, axis=0)
    upper_lagged = jnp.roll(ahead_sum, -block_size, axis=0)
    return new_store, lower_lagged, upper_lagged
```

```python
import functools

import jax
import jax.numpy as jnp
from jax import lax
from jax.experimental import pallas as pl
from jax.experimental.pallas import tpu as pltpu
from jax.sharding import PartitionSpec as P

MESH = pl.DeviceIdType.MESH
relax_rate = 0.3
LANES = 128
SUB = 8


def distances(ring):
    far = [ring // 2]
    for d in range(ring // 2 - 1, 0, -1):
        far += [d, ring - d]
    return far + [0]


def fourier_kernel(
    n_blk,
    n_harm,
    samples_hbm,
    store_hbm,
    phase,
    patch_row,
    harm_counts,
    freq_index,
    blade_counts,
    new_store,
    lower,
    upper,
    store,
    gathered,
    freq,
    rows,
    coef,
    mine,
    theirs,
    inbox,
    outbox,
    arrived,
    load_sem,
    pair_send,
    pair_recv,
    sum_send,
    sum_recv,
    ring_send,
    ring_recv,
    fwd_send,
    fwd_recv,
):
    slots, patches = store.shape[1], store.shape[2]
    row_count, slot_total = freq_index.shape
    ring = n_harm // 2
    share = patches // n_harm
    tiles = share // SUB
    blk = lax.axis_index("blk")
    harm = lax.axis_index("harm")
    chip, core = harm // 2, harm % 2
    partner = 2 * chip + 1 - core
    after = lax.rem(blk + 1, n_blk)
    before = lax.rem(blk + n_blk - 1, n_blk)
    hops = distances(ring)

    def peer(d):
        return 2 * lax.rem(chip + d, ring) + core

    barrier = pltpu.get_barrier_semaphore()
    pl.semaphore_signal(barrier, 1, device_id=(blk, partner), device_id_type=MESH)
    for d in hops:
        if d:
            pl.semaphore_signal(barrier, 1, device_id=(blk, peer(d)), device_id_type=MESH)
        for b in (after, before):
            pl.semaphore_signal(barrier, 1, device_id=(b, peer(d)), device_id_type=MESH)

    own = pltpu.make_async_copy(samples_hbm, gathered.at[harm], load_sem.at[2 * slots])
    own.start()
    loads = []
    for part in range(2):
        for j in range(slots):
            load = pltpu.make_async_copy(
                store_hbm.at[part, j], store.at[part, j], load_sem.at[part * slots + j]
            )
            load.start()
            loads.append(load)

    sub = lax.broadcasted_iota(jnp.int32, (SUB, LANES), 0)
    lane = lax.broadcasted_iota(jnp.int32, (SUB, LANES), 1)
    freq[...] = jnp.zeros((SUB, LANES), jnp.float32)
    freq[:row_count, :slot_total] = freq_index[...].astype(jnp.float32)
    frequency = freq[...]

    def by_row(ref, other):
        out = jnp.full((SUB, LANES), other)
        for r in range(row_count):
            out = jnp.where(sub == r, ref[r], out)
        return out

    now = frequency * by_row(phase, jnp.float32(0))
    blades = by_row(blade_counts, jnp.int32(1)).astype(jnp.float32)
    lag = 2.0 * jnp.pi * frequency / blades
    active = lane < by_row(harm_counts, jnp.int32(0))
    now_cos, now_sin = jnp.cos(now), jnp.sin(now)
    back, ahead = now - lag, now + lag
    back_cos, back_sin = jnp.cos(back), jnp.sin(back)
    ahead_cos, ahead_sin = jnp.cos(ahead), jnp.sin(ahead)
    gain = 2.0 * relax_rate
    keep = 1.0 - relax_rate
    zero = jnp.zeros((SUB, LANES), jnp.float32)

    def spread(table):
        return jnp.broadcast_to(jnp.sum(table, axis=1, keepdims=True), (SUB, LANES))

    for j in range(slots):
        here = lane == harm * slots + j
        on = active & here
        for i, table in enumerate((back_cos, back_sin, ahead_cos, ahead_sin)):
            coef[j, i] = spread(jnp.where(on, keep * table, zero))
        coef[j, 4] = spread(jnp.where(on, gain * now_cos, zero))
        coef[j, 5] = spread(jnp.where(on, gain * now_sin, zero))
        coef[j, 6] = spread(jnp.where(here, jnp.where(active, keep, 1.0), zero))
    back_gain = spread(jnp.where(active, gain * (now_cos * back_cos + now_sin * back_sin), zero))
    ahead_gain = spread(jnp.where(active, gain * (now_cos * ahead_cos + now_sin * ahead_sin), zero))

    for i in range(patches // LANES):
        line = jnp.broadcast_to(patch_row[i : i + 1, :], (LANES, LANES))
        rows[pl.ds(i * LANES, LANES), :] = line.T

    def pick(table, row):
        return jnp.take_along_axis(table, row, axis=0, mode="promise_in_bounds")

    for load in loads:
        load.wait()
    own.wait()

    tables = [[coef[j, i] for i in range(4)] for j in range(slots)]

    def partial(base):
        row = rows[pl.ds(base, SUB), :]
        back_sum, ahead_sum = zero, zero
        for j in range(slots):
            c, s = store[0, j, pl.ds(base, SUB), :], store[1, j, pl.ds(base, SUB), :]
            back_sum += pick(tables[j][0], row) * c + pick(tables[j][1], row) * s
            ahead_sum += pick(tables[j][2], row) * c + pick(tables[j][3], row) * s
        return back_sum, ahead_sum

    def target(k):
        step = jnp.where(lax.rem(k, 2) == 0, k // 2, ring - (k + 1) // 2)
        return lax.rem(chip + ring // 2 + step, ring)

    def partial_step(k, carry):
        first = target(k) * 2 * share
        for t in range(tiles):
            base = pl.multiple_of(first + (1 - core) * share + t * SUB, SUB)
            theirs[k, 0, pl.ds(t * SUB, SUB), :], theirs[k, 1, pl.ds(t * SUB, SUB), :] = partial(base)
        for t in range(tiles):
            base = pl.multiple_of(first + core * share + t * SUB, SUB)
            mine[k, 0, pl.ds(t * SUB, SUB), :], mine[k, 1, pl.ds(t * SUB, SUB), :] = partial(base)
        return carry

    lax.fori_loop(0, ring, partial_step, 0)
    for t in range(tiles):
        at = pl.ds(t * SUB, SUB)
        row = rows[pl.ds(pl.multiple_of(harm * share + t * SUB, SUB), SUB), :]
        value = gathered[harm, at, :]
        mine[ring - 1, 0, at, :] += pick(back_gain, row) * value
        mine[ring - 1, 1, at, :] += pick(ahead_gain, row) * value

    pl.semaphore_wait(barrier, 3 * ring)

    def remote(src, dst, send, recv, device):
        return pltpu.make_async_remote_copy(
            src_ref=src, dst_ref=dst, send_sem=send, recv_sem=recv, device_id=device, device_id_type=MESH
        )

    pair = [
        remote(theirs.at[k], inbox.at[k], pair_send.at[k], pair_recv.at[k], (blk, partner))
        for k in range(ring)
    ]
    around = [
        remote(gathered.at[harm], gathered.at[harm], ring_send.at[k], ring_recv.at[k], (blk, peer(hops[k])))
        for k in range(ring - 1)
    ]
    sums = [
        [
            remote(outbox.at[k, i], arrived.at[k, i], sum_send.at[k, i], sum_recv.at[k, i], (b, peer(hops[k])))
            for i, b in enumerate((after, before))
        ]
        for k in range(ring)
    ]
    forward = []
    for k in range(ring):
        source = gathered.at[peer(ring - hops[k])]
        forward.append(remote(source, source, fwd_send.at[k], fwd_recv.at[k], (blk, partner)))

    pair[0].start()
    pair[1].start()
    for k in range(ring - 1):
        around[k].start()
    for k in range(2, ring):
        pair[k].start()
    forward[ring - 1].start()
    for k in range(ring):
        pair[k].wait_recv()
        outbox[k] = mine[k] + inbox[k]
        if k:
            for copy in sums[k - 1]:
                copy.start()

    for k in range(ring - 2, -1, -1):
        around[k].wait_recv()
        forward[k].start()
        if k == ring - 2:
            for copy in sums[ring - 1]:
                copy.start()
    for k in range(ring - 1, -1, -1):
        forward[k].wait_recv()

    def update_step(i, carry):
        for t in range(tiles):
            at = pl.ds(pl.multiple_of(i * share + t * SUB, SUB), SUB)
            row = rows[at, :]
            value = gathered[i, pl.ds(t * SUB, SUB), :]
            for j in range(slots):
                hold = pick(coef[j, 6], row)
                new_store[0, j, at, :] = hold * store[0, j, at, :] + pick(coef[j, 4], row) * value
                new_store[1, j, at, :] = hold * store[1, j, at, :] + pick(coef[j, 5], row) * value
        return carry

    lax.fori_loop(0, n_harm, update_step, 0)

    for i, out in enumerate((lower, upper)):
        total = None
        for k in range(ring - 1, -1, -1):
            sums[k][i].wait_recv()
            total = arrived[k, i] if total is None else total + arrived[k, i]
        out[...] = total
    for k in range(ring):
        pair[k].wait_send()
        forward[k].wait_send()
        if k < ring - 1:
            around[k].wait_send()
        for copy in sums[k]:
            copy.wait_send()


def write_kernel(a, b, c, a_out, b_out, c_out, sems):
    copies = [
        pltpu.make_async_copy(src, dst, sems.at[i])
        for i, (src, dst) in enumerate(((a, a_out), (b, b_out), (c, c_out)))
    ]
    for copy in copies:
        copy.start()
    for copy in copies:
        copy.wait()


def solution(mesh):
    n_blk, n_harm = mesh.shape["blk"], mesh.shape["harm"]
    ring = n_harm // 2

    def shards(samples, store, phase, patch_row, harm_counts, freq_index, blade_counts):
        share, points = samples.shape
        _, slots, patches, _ = store.shape
        f32 = jnp.float32
        any_spec = pl.BlockSpec(memory_space=pl.ANY)
        smem = pl.BlockSpec(memory_space=pltpu.SMEM)
        vmem = pl.BlockSpec(memory_space=pltpu.VMEM)
        dma = pltpu.SemaphoreType.DMA
        outs = (
            pltpu.VMEM(store.shape, f32),
            pltpu.VMEM(samples.shape, f32),
            pltpu.VMEM(samples.shape, f32),
        )
        block = (ring, 2, share, points)
        results = pl.pallas_call(
            functools.partial(fourier_kernel, n_blk, n_harm),
            name="fourier",
            out_shape=outs,
            in_specs=[any_spec, any_spec, smem, vmem, smem, vmem, smem],
            out_specs=[vmem, vmem, vmem],
            scratch_shapes=[
                pltpu.VMEM(store.shape, f32),
                pltpu.VMEM((n_harm, share, points), f32),
                pltpu.VMEM((SUB, LANES), f32),
                pltpu.VMEM((patches, LANES), jnp.int32),
                pltpu.VMEM((slots, 7, SUB, LANES), f32),
                pltpu.VMEM(block, f32),
                pltpu.VMEM(block, f32),
                pltpu.VMEM(block, f32),
                pltpu.VMEM(block, f32),
                pltpu.VMEM(block, f32),
                dma((2 * slots + 1,)),
                dma((ring,)),
                dma((ring,)),
                dma((ring, 2)),
                dma((ring, 2)),
                dma((ring - 1,)),
                dma((ring - 1,)),
                dma((ring,)),
                dma((ring,)),
            ],
            compiler_params=pltpu.CompilerParams(collective_id=0, has_side_effects=True),
        )(
            samples,
            store,
            phase,
            patch_row.reshape(patches // LANES, LANES),
            harm_counts,
            freq_index,
            blade_counts,
        )
        results = [pltpu.with_memory_space_constraint(r, pltpu.VMEM) for r in results]
        return pl.pallas_call(
            write_kernel,
            name="write",
            out_shape=tuple(jax.ShapeDtypeStruct(o.shape, f32) for o in outs),
            in_specs=[vmem, vmem, vmem],
            out_specs=[any_spec, any_spec, any_spec],
            scratch_shapes=[dma((3,))],
        )(*results)

    in_specs = (P(("blk", "harm"), None), P(None, "harm", "blk", None), P(), P("blk"), P(), P(), P())
    out_specs = (P(None, "harm", "blk", None), P(("blk", "harm"), None), P(("blk", "harm"), None))
    return jax.shard_map(shards, mesh=mesh, in_specs=in_specs, out_specs=out_specs, check_vma=False)
```

```python
import functools

import jax
import jax.numpy as jnp
from jax import lax
from jax.experimental import pallas as pl
from jax.experimental.pallas import tpu as pltpu
from jax.sharding import PartitionSpec as P

MESH = pl.DeviceIdType.MESH
relax_rate = 0.3
LANES = 128
SUB = 8


HOPS = (3, 5, 4, 2, 6, 1, 7, 0)


def fourier_kernel(
    n_blk,
    n_harm,
    samples_hbm,
    store_hbm,
    phase_hbm,
    patch_row_hbm,
    harm_counts_hbm,
    freq_index_hbm,
    blade_counts_hbm,
    new_store,
    lower,
    upper,
    store,
    gathered,
    freq,
    rows,
    coef,
    mine,
    theirs,
    inbox,
    outbox,
    passing,
    arrived,
    phase,
    harm_counts,
    blade_counts,
    patch_row,
    freq_index,
    beyond,
    small_sem,
    own_sem,
    load_sem,
    pair_send,
    pair_recv,
    pass_send,
    pass_recv,
    sum_send,
    sum_recv,
    ring_send,
    ring_recv,
    fwd_send,
    fwd_recv,
):
    slots, patches = store.shape[1], store.shape[2]
    row_count, slot_total = freq_index.shape
    ring = n_harm // 2
    share = patches // n_harm
    tiles = share // SUB
    blk = lax.axis_index("blk")
    harm = lax.axis_index("harm")
    chip, core = harm // 2, harm % 2
    partner = 2 * chip + 1 - core
    after = lax.rem(blk + 1, n_blk)
    before = lax.rem(blk + n_blk - 1, n_blk)

    def signal(sem, b, h):
        pl.semaphore_signal(sem, 1, device_id=(b, h), device_id_type=MESH)

    def remote(src, dst, send, recv, device):
        return pltpu.make_async_remote_copy(
            src_ref=src, dst_ref=dst, send_sem=send, recv_sem=recv, device_id=device, device_id_type=MESH
        )

    def peer(d):
        return 2 * lax.rem(chip + d, ring) + core

    def peer(d):
        return 2 * lax.rem(chip + d, ring) + core

    barrier = pltpu.get_barrier_semaphore()
    for d in (2, 6, 1, 7):
        signal(barrier, blk, peer(d))
    for b, h in ((after, harm), (before, harm), (blk, partner)):
        signal(barrier, b, h)

    small = []
    for i, (src, dst) in enumerate(
        (
            (phase_hbm, phase),
            (harm_counts_hbm, harm_counts),
            (blade_counts_hbm, blade_counts),
            (freq_index_hbm, freq_index),
            (patch_row_hbm, patch_row),
        )
    ):
        small.append(pltpu.make_async_copy(src, dst, small_sem.at[i]))
        small[-1].start()

    def chip_at(k):
        return lax.rem(chip + HOPS[k], ring)

    loads = []
    for k in range(ring):
        at = pl.ds(pl.multiple_of(chip_at(k) * 2 * share, 2 * share), 2 * share)
        loads.append(pltpu.make_async_copy(store_hbm.at[:, :, at], store.at[:, :, at], load_sem.at[k]))
        loads[-1].start()
    own = pltpu.make_async_copy(samples_hbm, gathered.at[harm], own_sem)
    own.start()

    for copy in small:
        copy.wait()
    sub = lax.broadcasted_iota(jnp.int32, (SUB, LANES), 0)
    lane = lax.broadcasted_iota(jnp.int32, (SUB, LANES), 1)
    freq[...] = jnp.zeros((SUB, LANES), jnp.float32)
    freq[:row_count, :slot_total] = freq_index[...].astype(jnp.float32)
    frequency = freq[...]

    def by_row(ref, other):
        out = jnp.full((SUB, LANES), other)
        for r in range(row_count):
            out = jnp.where(sub == r, ref[r], out)
        return out

    now = frequency * by_row(phase, jnp.float32(0))
    blades = by_row(blade_counts, jnp.int32(1)).astype(jnp.float32)
    lag = 2.0 * jnp.pi * frequency / blades
    active = lane < by_row(harm_counts, jnp.int32(0))
    now_cos, now_sin = jnp.cos(now), jnp.sin(now)
    back, ahead = now - lag, now + lag
    back_cos, back_sin = jnp.cos(back), jnp.sin(back)
    ahead_cos, ahead_sin = jnp.cos(ahead), jnp.sin(ahead)
    gain = 2.0 * relax_rate
    keep = 1.0 - relax_rate
    zero = jnp.zeros((SUB, LANES), jnp.float32)

    def spread(table):
        return jnp.broadcast_to(jnp.sum(table, axis=1, keepdims=True), (SUB, LANES))

    for j in range(slots):
        here = lane == harm * slots + j
        on = active & here
        for i, table in enumerate((back_cos, back_sin, ahead_cos, ahead_sin)):
            coef[j, i] = spread(jnp.where(on, keep * table, zero))
        coef[j, 4] = spread(jnp.where(on, gain * now_cos, zero))
        coef[j, 5] = spread(jnp.where(on, gain * now_sin, zero))
        coef[j, 6] = spread(jnp.where(here, jnp.where(active, keep, 1.0), zero))
    back_gain = spread(jnp.where(active, gain * (now_cos * back_cos + now_sin * back_sin), zero))
    ahead_gain = spread(jnp.where(active, gain * (now_cos * ahead_cos + now_sin * ahead_sin), zero))

    for i in range(patches // LANES):
        line = jnp.broadcast_to(patch_row[i : i + 1, :], (LANES, LANES))
        rows[pl.ds(i * LANES, LANES), :] = line.T

    def pick(table, row):
        return jnp.take_along_axis(table, row, axis=0, mode="promise_in_bounds")

    tables = [[coef[j, i] for i in range(4)] for j in range(slots)]

    def partial(base):
        row = rows[pl.ds(base, SUB), :]
        back_sum, ahead_sum = zero, zero
        for j in range(slots):
            c, s = store[0, j, pl.ds(base, SUB), :], store[1, j, pl.ds(base, SUB), :]
            back_sum += pick(tables[j][0], row) * c + pick(tables[j][1], row) * s
            ahead_sum += pick(tables[j][2], row) * c + pick(tables[j][3], row) * s
        return back_sum, ahead_sum

    def step_chip(k):
        d = jnp.where(k < 2, 3 + 2 * k, jnp.where(k == 2, 4, jnp.where(k == 7, 0, 0)))
        d = jnp.where(k == 3, 2, jnp.where(k == 4, 6, jnp.where(k == 5, 1, jnp.where(k == 6, 7, d))))
        return lax.rem(chip + d, ring)

    def pair_copy(k):
        return remote(theirs.at[k], inbox.at[k], pair_send, pair_recv.at[k], (blk, partner))

    def partial_step(k, carry):
        at = pl.ds(pl.multiple_of(step_chip(k) * 2 * share, 2 * share), 2 * share)
        pltpu.make_async_copy(store_hbm.at[:, :, at], store.at[:, :, at], load_sem.at[k]).wait()
        first = step_chip(k) * 2 * share
        for t in range(tiles):
            base = pl.multiple_of(first + (1 - core) * share + t * SUB, SUB)
            theirs[k, 0, pl.ds(t * SUB, SUB), :], theirs[k, 1, pl.ds(t * SUB, SUB), :] = partial(base)
        for t in range(tiles):
            base = pl.multiple_of(first + core * share + t * SUB, SUB)
            mine[k, 0, pl.ds(t * SUB, SUB), :], mine[k, 1, pl.ds(t * SUB, SUB), :] = partial(base)
        return carry

    lax.fori_loop(0, ring, partial_step, 0)
    own.wait()

    def update(h):
        for t in range(tiles):
            at = pl.ds(pl.multiple_of(h * share + t * SUB, SUB), SUB)
            row = rows[at, :]
            value = gathered[h, pl.ds(t * SUB, SUB), :]
            for j in range(slots):
                hold = pick(coef[j, 6], row)
                new_store[0, j, at, :] = hold * store[0, j, at, :] + pick(coef[j, 4], row) * value
                new_store[1, j, at, :] = hold * store[1, j, at, :] + pick(coef[j, 5], row) * value

    pl.semaphore_wait(barrier, 7)
    signal(beyond, after, harm)
    signal(beyond, before, harm)

    def place(d):
        return gathered.at[peer(d)]

    def block_to(d, recv):
        return remote(samples_hbm, place(0), ring_send, ring_recv.at[recv], (blk, peer(d)))

    def forward(slot, d):
        return remote(place(d) if d else samples_hbm, place(d), fwd_send, fwd_recv.at[slot], (blk, partner))

    for k in range(3):
        pair_copy(k).start()
    block_to(2, 2).start()
    block_to(6, 3).start()
    for k in range(3, ring):
        pair_copy(k).start()
    forward(0, 0).start()

    def sums_to(k):
        for i, b in enumerate((after, before)):
            source, target = outbox.at[k, i], arrived.at[k - 3, i]
            remote(source, target, sum_send, sum_recv, (b, peer(HOPS[k]))).start()

    def far(k):
        if k < 2:
            at = pl.ds(2 * k, 2)
            sem = pass_recv.at[k]
            remote(outbox.at[k], passing.at[at], pass_send, sem, (blk, peer((1, 7)[k]))).start()
        else:
            pass_back.start()
            pass_ahead.start()

    pass_back = remote(outbox.at[2, 0], passing.at[4], pass_send, pass_recv.at[2], (blk, peer(2)))
    pass_ahead = remote(outbox.at[2, 1], passing.at[5], pass_send, pass_recv.at[3], (blk, peer(6)))

    update(harm)
    for k in range(ring - 1):
        pair_copy(k).wait_recv()
        outbox[k] = mine[k] + inbox[k]
        if 1 <= k <= 3:
            far(k - 1)
        if k == 3:
            block_to(1, 0).start()
            block_to(7, 1).start()
    pair_copy(ring - 1).wait_recv()
    for t in range(tiles):
        at = pl.ds(t * SUB, SUB)
        row = rows[pl.ds(pl.multiple_of(harm * share + t * SUB, SUB), SUB), :]
        value = gathered[harm, at, :]
        k = ring - 1
        outbox[k, 0, at, :] = mine[k, 0, at, :] + inbox[k, 0, at, :] + pick(back_gain, row) * value
        outbox[k, 1, at, :] = mine[k, 1, at, :] + inbox[k, 1, at, :] + pick(ahead_gain, row) * value

    top, bottom = pl.ds(0, share // 2), pl.ds(share // 2, share // 2)

    def relay(src, slot, d):
        return remote(src, src, ring_send, ring_recv.at[slot], (blk, peer(d)))

    block_to(2, 2).wait_recv()
    relay(place(6), 4, 1).start()
    relay(place(6).at[top], 6, 2).start()
    block_to(6, 3).wait_recv()
    relay(place(2), 5, 7).start()
    relay(place(2).at[bottom], 7, 6).start()
    forward(1, 6).start()
    forward(2, 2).start()

    pl.semaphore_wait(beyond, 2)
    for k in (5, 6, 7):
        sums_to(k)

    def received(ref, sem):
        pltpu.make_async_copy(ref, ref, sem).wait()

    received(passing.at[pl.ds(0, 2)], pass_recv.at[0])
    received(passing.at[4], pass_recv.at[2])
    outbox[3, 0] = outbox[3, 0] + passing[0] + passing[4]
    outbox[3, 1] = outbox[3, 1] + passing[1]
    received(passing.at[pl.ds(2, 2)], pass_recv.at[1])
    received(passing.at[5], pass_recv.at[3])
    outbox[4, 0] = outbox[4, 0] + passing[2]
    outbox[4, 1] = outbox[4, 1] + passing[3] + passing[5]
    sums_to(3)
    update(peer(6))
    sums_to(4)
    update(peer(2))
    block_to(1, 0).wait_recv()
    forward(3, 7).start()
    block_to(7, 1).wait_recv()
    forward(4, 1).start()
    update(peer(7))
    update(peer(1))

    received(place(5), ring_recv.at[4])
    forward(5, 5).start()
    received(place(3), ring_recv.at[5])
    forward(6, 3).start()
    received(place(4).at[top], ring_recv.at[6])
    received(place(4).at[bottom], ring_recv.at[7])
    forward(7, 4).start()
    for d in (5, 3, 4):
        update(peer(d))
    for slot, d in enumerate((0, 6, 2, 7, 1, 5, 3, 4)):
        h = 2 * lax.rem(chip + d, ring) + 1 - core
        received(gathered.at[h], fwd_recv.at[slot])
        update(h)

    received(arrived, sum_recv)
    for i, out in enumerate((lower, upper)):
        total = arrived[0, i]
        for k in range(1, arrived.shape[0]):
            total += arrived[k, i]
        out[...] = total
    received(theirs, pair_send)
    received(outbox.at[pl.ds(0, 3)], pass_send)
    received(arrived, sum_send)
    received(gathered.at[pl.ds(0, 7)], ring_send)
    received(gathered.at[pl.ds(0, ring)], fwd_send)


def write_kernel(a, b, c, a_out, b_out, c_out, sems):
    copies = [
        pltpu.make_async_copy(src, dst, sems.at[i])
        for i, (src, dst) in enumerate(((a, a_out), (b, b_out), (c, c_out)))
    ]
    for copy in copies:
        copy.start()
    for copy in copies:
        copy.wait()


def solution(mesh):
    n_blk, n_harm = mesh.shape["blk"], mesh.shape["harm"]
    ring = n_harm // 2

    def shards(samples, store, phase, patch_row, harm_counts, freq_index, blade_counts):
        share, points = samples.shape
        _, slots, patches, _ = store.shape
        f32 = jnp.float32
        any_spec = pl.BlockSpec(memory_space=pl.ANY)
        vmem = pl.BlockSpec(memory_space=pltpu.VMEM)
        dma = pltpu.SemaphoreType.DMA
        outs = (
            pltpu.VMEM(store.shape, f32),
            pltpu.VMEM(samples.shape, f32),
            pltpu.VMEM(samples.shape, f32),
        )
        block = (ring, 2, share, points)
        results = pl.pallas_call(
            functools.partial(fourier_kernel, n_blk, n_harm),
            name="fourier",
            out_shape=outs,
            in_specs=[any_spec] * 7,
            out_specs=[vmem, vmem, vmem],
            scratch_shapes=[
                pltpu.VMEM(store.shape, f32),
                pltpu.VMEM((n_harm, share, points), f32),
                pltpu.VMEM((SUB, LANES), f32),
                pltpu.VMEM((patches, LANES), jnp.int32),
                pltpu.VMEM((slots, 7, SUB, LANES), f32),
                pltpu.VMEM(block, f32),
                pltpu.VMEM(block, f32),
                pltpu.VMEM(block, f32),
                pltpu.VMEM(block, f32),
                pltpu.VMEM((6, share, points), f32),
                pltpu.VMEM((5, 2, share, points), f32),
                pltpu.SMEM(phase.shape, f32),
                pltpu.SMEM(harm_counts.shape, jnp.int32),
                pltpu.SMEM(blade_counts.shape, jnp.int32),
                pltpu.VMEM((patches // LANES, LANES), jnp.int32),
                pltpu.VMEM(freq_index.shape, jnp.int32),
                pltpu.SemaphoreType.REGULAR,
                dma((5,)),
                dma(()),
                dma((ring,)),
                dma(()),
                dma((ring,)),
                dma(()),
                dma((4,)),
                dma(()),
                dma(()),
                dma(()),
                dma((8,)),
                dma(()),
                dma((ring,)),
            ],
            compiler_params=pltpu.CompilerParams(collective_id=0, has_side_effects=True),
        )(
            samples,
            store,
            phase,
            patch_row.reshape(patches // LANES, LANES),
            harm_counts,
            freq_index,
            blade_counts,
        )
        results = [pltpu.with_memory_space_constraint(r, pltpu.VMEM) for r in results]
        return pl.pallas_call(
            write_kernel,
            name="write",
            out_shape=tuple(jax.ShapeDtypeStruct(o.shape, f32) for o in outs),
            in_specs=[vmem, vmem, vmem],
            out_specs=[any_spec, any_spec, any_spec],
            scratch_shapes=[dma((3,))],
        )(*results)

    in_specs = (P(("blk", "harm"), None), P(None, "harm", "blk", None), P(), P("blk"), P(), P(), P())
    out_specs = (P(None, "harm", "blk", None), P(("blk", "harm"), None), P(("blk", "harm"), None))
    return jax.shard_map(shards, mesh=mesh, in_specs=in_specs, out_specs=out_specs, check_vma=False)
```

```python
import functools

import jax
import jax.numpy as jnp
from jax import lax
from jax.experimental import pallas as pl
from jax.experimental.pallas import tpu as pltpu
from jax.sharding import PartitionSpec as P

MESH = pl.DeviceIdType.MESH
relax_rate = 0.3
LANES = 128
SUB = 8


HOPS = (4, 3, 5, 2, 6, 1, 7, 0)


def fourier_kernel(
    n_blk,
    n_harm,
    samples_hbm,
    store_hbm,
    phase_hbm,
    patch_row_hbm,
    harm_counts_hbm,
    freq_index_hbm,
    blade_counts_hbm,
    new_store,
    lower,
    upper,
    store,
    gathered,
    freq,
    rows,
    coef,
    mine,
    theirs,
    inbox,
    outbox,
    passing,
    arrived,
    phase,
    harm_counts,
    blade_counts,
    patch_row,
    freq_index,
    around,
    beyond,
    small_sem,
    own_sem,
    load_sem,
    pair_send,
    pair_recv,
    pass_send,
    pass_recv,
    sum_send,
    sum_recv,
    ring_send,
    ring_recv,
    fwd_send,
    fwd_recv,
):
    slots, patches = store.shape[1], store.shape[2]
    row_count, slot_total = freq_index.shape
    ring = n_harm // 2
    share = patches // n_harm
    tiles = share // SUB
    blk = lax.axis_index("blk")
    harm = lax.axis_index("harm")
    chip, core = harm // 2, harm % 2
    partner = 2 * chip + 1 - core
    after = lax.rem(blk + 1, n_blk)
    before = lax.rem(blk + n_blk - 1, n_blk)

    def signal(sem, b, h):
        pl.semaphore_signal(sem, 1, device_id=(b, h), device_id_type=MESH)

    def remote(src, dst, send, recv, device):
        return pltpu.make_async_remote_copy(
            src_ref=src, dst_ref=dst, send_sem=send, recv_sem=recv, device_id=device, device_id_type=MESH
        )

    def peer(d):
        return 2 * lax.rem(chip + d, ring) + core

    def peer(d):
        return 2 * lax.rem(chip + d, ring) + core

    barrier = pltpu.get_barrier_semaphore()
    for d in (2, 6, 1, 7):
        signal(barrier, blk, peer(d) - core)
    signal(barrier, after, 2 * chip + 1)
    signal(barrier, before, 2 * chip + 1)

    @pl.when(core == 1)
    def _():
        signal(barrier, blk, partner)

    small = []
    for i, (src, dst) in enumerate(
        (
            (phase_hbm, phase),
            (harm_counts_hbm, harm_counts),
            (blade_counts_hbm, blade_counts),
            (freq_index_hbm, freq_index),
            (patch_row_hbm, patch_row),
        )
    ):
        small.append(pltpu.make_async_copy(src, dst, small_sem.at[i]))
        small[-1].start()

    def chip_at(k):
        return lax.rem(chip + HOPS[k], ring)

    loads = []
    for k in range(ring):
        at = pl.ds(pl.multiple_of(chip_at(k) * 2 * share, 2 * share), 2 * share)
        loads.append(pltpu.make_async_copy(store_hbm.at[:, :, at], store.at[:, :, at], load_sem.at[k]))
        if k < 3:
            loads[-1].start()
    own = pltpu.make_async_copy(samples_hbm, gathered.at[harm], own_sem)
    own.start()

    for copy in small:
        copy.wait()
    for k in range(3, ring):
        loads[k].start()
    sub = lax.broadcasted_iota(jnp.int32, (SUB, LANES), 0)
    lane = lax.broadcasted_iota(jnp.int32, (SUB, LANES), 1)
    freq[...] = jnp.zeros((SUB, LANES), jnp.float32)
    freq[:row_count, :slot_total] = freq_index[...].astype(jnp.float32)
    frequency = freq[...]

    def by_row(ref, other):
        out = jnp.full((SUB, LANES), other)
        for r in range(row_count):
            out = jnp.where(sub == r, ref[r], out)
        return out

    now = frequency * by_row(phase, jnp.float32(0))
    blades = by_row(blade_counts, jnp.int32(1)).astype(jnp.float32)
    lag = 2.0 * jnp.pi * frequency / blades
    active = lane < by_row(harm_counts, jnp.int32(0))
    now_cos, now_sin = jnp.cos(now), jnp.sin(now)
    back, ahead = now - lag, now + lag
    back_cos, back_sin = jnp.cos(back), jnp.sin(back)
    ahead_cos, ahead_sin = jnp.cos(ahead), jnp.sin(ahead)
    gain = 2.0 * relax_rate
    keep = 1.0 - relax_rate
    zero = jnp.zeros((SUB, LANES), jnp.float32)

    def spread(table):
        return jnp.broadcast_to(jnp.sum(table, axis=1, keepdims=True), (SUB, LANES))

    for j in range(slots):
        here = lane == harm * slots + j
        on = active & here
        for i, table in enumerate((back_cos, back_sin, ahead_cos, ahead_sin)):
            coef[j, i] = spread(jnp.where(on, keep * table, zero))
        coef[j, 4] = spread(jnp.where(on, gain * now_cos, zero))
        coef[j, 5] = spread(jnp.where(on, gain * now_sin, zero))
        coef[j, 6] = spread(jnp.where(here, jnp.where(active, keep, 1.0), zero))
    back_gain = spread(jnp.where(active, gain * (now_cos * back_cos + now_sin * back_sin), zero))
    ahead_gain = spread(jnp.where(active, gain * (now_cos * ahead_cos + now_sin * ahead_sin), zero))

    for i in range(patches // LANES):
        line = jnp.broadcast_to(patch_row[i : i + 1, :], (LANES, LANES))
        rows[pl.ds(i * LANES, LANES), :] = line.T

    def pick(table, row):
        return jnp.take_along_axis(table, row, axis=0, mode="promise_in_bounds")

    tables = [[coef[j, i] for i in range(4)] for j in range(slots)]

    def partial(base):
        row = rows[pl.ds(base, SUB), :]
        back_sum, ahead_sum = zero, zero
        for j in range(slots):
            c, s = store[0, j, pl.ds(base, SUB), :], store[1, j, pl.ds(base, SUB), :]
            back_sum += pick(tables[j][0], row) * c + pick(tables[j][1], row) * s
            ahead_sum += pick(tables[j][2], row) * c + pick(tables[j][3], row) * s
        return back_sum, ahead_sum

    def step_chip(k):
        step = jnp.where(lax.rem(k, 2) == 0, k // 2, ring - (k + 1) // 2)
        return lax.rem(chip + ring // 2 + step, ring)

    def pair_copy(k):
        return remote(theirs.at[k], inbox.at[k], pair_send, pair_recv.at[k], (blk, partner))

    def partial_step(k, carry):
        at = pl.ds(pl.multiple_of(step_chip(k) * 2 * share, 2 * share), 2 * share)
        pltpu.make_async_copy(store_hbm.at[:, :, at], store.at[:, :, at], load_sem.at[k]).wait()
        first = step_chip(k) * 2 * share
        for t in range(tiles):
            base = pl.multiple_of(first + (1 - core) * share + t * SUB, SUB)
            theirs[k, 0, pl.ds(t * SUB, SUB), :], theirs[k, 1, pl.ds(t * SUB, SUB), :] = partial(base)
        for t in range(tiles):
            base = pl.multiple_of(first + core * share + t * SUB, SUB)
            mine[k, 0, pl.ds(t * SUB, SUB), :], mine[k, 1, pl.ds(t * SUB, SUB), :] = partial(base)
        return carry

    lax.fori_loop(0, 3, partial_step, 0)

    def update(h):
        for t in range(tiles):
            at = pl.ds(pl.multiple_of(h * share + t * SUB, SUB), SUB)
            row = rows[at, :]
            value = gathered[h, pl.ds(t * SUB, SUB), :]
            for j in range(slots):
                hold = pick(coef[j, 6], row)
                new_store[0, j, at, :] = hold * store[0, j, at, :] + pick(coef[j, 4], row) * value
                new_store[1, j, at, :] = hold * store[1, j, at, :] + pick(coef[j, 5], row) * value

    @pl.when(core == 0)
    def _():
        pl.semaphore_wait(barrier, 9)
        signal(around, blk, partner)

    @pl.when(core == 1)
    def _():
        pl.semaphore_wait(around, 1)

    def place(d):
        return gathered.at[peer(d)]

    def block_to(d, recv):
        return remote(samples_hbm, place(0), ring_send, ring_recv.at[recv], (blk, peer(d)))

    def forward(slot, d):
        return remote(place(d) if d else samples_hbm, place(d), fwd_send, fwd_recv.at[slot], (blk, partner))

    for k in range(3):
        pair_copy(k).start()
    block_to(2, 2).start()
    block_to(6, 3).start()
    forward(0, 0).start()
    lax.fori_loop(3, ring, partial_step, 0)

    def sums_to(k):
        for i, b in enumerate((after, before)):
            source, target = outbox.at[k, i], arrived.at[k - 3, i]
            remote(source, target, sum_send, sum_recv, (b, peer(HOPS[k]))).start()

    def far(k):
        if k:
            at = pl.ds(2 * k - 2, 2)
            sem = pass_recv.at[k - 1]
            remote(outbox.at[k], passing.at[at], pass_send, sem, (blk, peer((1, 7)[k - 1]))).start()
        else:
            pass_back.start()
            pass_ahead.start()

    pass_back = remote(outbox.at[0, 0], passing.at[4], pass_send, pass_recv.at[2], (blk, peer(2)))
    pass_ahead = remote(outbox.at[0, 1], passing.at[5], pass_send, pass_recv.at[3], (blk, peer(6)))

    for k in range(3):
        pair_copy(k).wait_recv()
        outbox[k] = mine[k] + inbox[k]
        if k:
            far(k - 1)
    for k in range(3, ring):
        pair_copy(k).start()
    far(2)
    block_to(1, 0).start()
    block_to(7, 1).start()
    own.wait()
    update(harm)
    for k in range(3, ring - 1):
        pair_copy(k).wait_recv()
        outbox[k] = mine[k] + inbox[k]
    pair_copy(ring - 1).wait_recv()
    for t in range(tiles):
        at = pl.ds(t * SUB, SUB)
        row = rows[pl.ds(pl.multiple_of(harm * share + t * SUB, SUB), SUB), :]
        value = gathered[harm, at, :]
        k = ring - 1
        outbox[k, 0, at, :] = mine[k, 0, at, :] + inbox[k, 0, at, :] + pick(back_gain, row) * value
        outbox[k, 1, at, :] = mine[k, 1, at, :] + inbox[k, 1, at, :] + pick(ahead_gain, row) * value

    @pl.when(core == 1)
    def _():
        pl.semaphore_wait(barrier, 4)
        for b in (after, before):
            signal(beyond, b, 2 * chip)
            signal(beyond, b, 2 * chip + 1)

    top, bottom = pl.ds(0, share // 2), pl.ds(share // 2, share // 2)

    def relay(src, slot, d):
        return remote(src, src, ring_send, ring_recv.at[slot], (blk, peer(d)))

    block_to(2, 2).wait_recv()
    relay(place(6), 4, 1).start()
    relay(place(6).at[top], 6, 2).start()
    block_to(6, 3).wait_recv()
    relay(place(2), 5, 7).start()
    relay(place(2).at[bottom], 7, 6).start()
    forward(1, 6).start()
    forward(2, 2).start()

    pl.semaphore_wait(beyond, 2)
    for k in (5, 6, 7):
        sums_to(k)

    def received(ref, sem):
        pltpu.make_async_copy(ref, ref, sem).wait()

    received(passing.at[pl.ds(0, 2)], pass_recv.at[0])
    received(passing.at[4], pass_recv.at[2])
    outbox[3, 0] = outbox[3, 0] + passing[0] + passing[4]
    outbox[3, 1] = outbox[3, 1] + passing[1]
    received(passing.at[pl.ds(2, 2)], pass_recv.at[1])
    received(passing.at[5], pass_recv.at[3])
    outbox[4, 0] = outbox[4, 0] + passing[2]
    outbox[4, 1] = outbox[4, 1] + passing[3] + passing[5]
    sums_to(3)
    update(peer(6))
    sums_to(4)
    update(peer(2))
    block_to(1, 0).wait_recv()
    forward(3, 7).start()
    block_to(7, 1).wait_recv()
    forward(4, 1).start()
    update(peer(7))
    update(peer(1))

    received(place(5), ring_recv.at[4])
    forward(5, 5).start()
    received(place(3), ring_recv.at[5])
    forward(6, 3).start()
    received(place(4).at[top], ring_recv.at[6])
    received(place(4).at[bottom], ring_recv.at[7])
    forward(7, 4).start()
    for d in (5, 3, 4):
        update(peer(d))
    for slot, d in enumerate((0, 6, 2, 7, 1, 5, 3, 4)):
        h = 2 * lax.rem(chip + d, ring) + 1 - core
        received(gathered.at[h], fwd_recv.at[slot])
        update(h)

    received(arrived, sum_recv)
    for i, out in enumerate((lower, upper)):
        total = arrived[0, i]
        for k in range(1, arrived.shape[0]):
            total += arrived[k, i]
        out[...] = total
    received(theirs, pair_send)
    received(outbox.at[pl.ds(0, 3)], pass_send)
    received(arrived, sum_send)
    received(gathered.at[pl.ds(0, 7)], ring_send)
    received(gathered.at[pl.ds(0, ring)], fwd_send)


def write_kernel(a, b, c, a_out, b_out, c_out, sems):
    copies = [
        pltpu.make_async_copy(src, dst, sems.at[i])
        for i, (src, dst) in enumerate(((a, a_out), (b, b_out), (c, c_out)))
    ]
    for copy in copies:
        copy.start()
    for copy in copies:
        copy.wait()


def solution(mesh):
    n_blk, n_harm = mesh.shape["blk"], mesh.shape["harm"]
    ring = n_harm // 2

    def shards(samples, store, phase, patch_row, harm_counts, freq_index, blade_counts):
        share, points = samples.shape
        _, slots, patches, _ = store.shape
        f32 = jnp.float32
        any_spec = pl.BlockSpec(memory_space=pl.ANY)
        vmem = pl.BlockSpec(memory_space=pltpu.VMEM)
        dma = pltpu.SemaphoreType.DMA
        outs = (
            pltpu.VMEM(store.shape, f32),
            pltpu.VMEM(samples.shape, f32),
            pltpu.VMEM(samples.shape, f32),
        )
        block = (ring, 2, share, points)
        results = pl.pallas_call(
            functools.partial(fourier_kernel, n_blk, n_harm),
            name="fourier",
            out_shape=outs,
            in_specs=[any_spec] * 7,
            out_specs=[vmem, vmem, vmem],
            scratch_shapes=[
                pltpu.VMEM(store.shape, f32),
                pltpu.VMEM((n_harm, share, points), f32),
                pltpu.VMEM((SUB, LANES), f32),
                pltpu.VMEM((patches, LANES), jnp.int32),
                pltpu.VMEM((slots, 7, SUB, LANES), f32),
                pltpu.VMEM(block, f32),
                pltpu.VMEM(block, f32),
                pltpu.VMEM(block, f32),
                pltpu.VMEM(block, f32),
                pltpu.VMEM((6, share, points), f32),
                pltpu.VMEM((5, 2, share, points), f32),
                pltpu.SMEM(phase.shape, f32),
                pltpu.SMEM(harm_counts.shape, jnp.int32),
                pltpu.SMEM(blade_counts.shape, jnp.int32),
                pltpu.VMEM((patches // LANES, LANES), jnp.int32),
                pltpu.VMEM(freq_index.shape, jnp.int32),
                pltpu.SemaphoreType.REGULAR,
                pltpu.SemaphoreType.REGULAR,
                dma((5,)),
                dma(()),
                dma((ring,)),
                dma(()),
                dma((ring,)),
                dma(()),
                dma((4,)),
                dma(()),
                dma(()),
                dma(()),
                dma((8,)),
                dma(()),
                dma((ring,)),
            ],
            compiler_params=pltpu.CompilerParams(collective_id=0, has_side_effects=True),
        )(
            samples,
            store,
            phase,
            patch_row.reshape(patches // LANES, LANES),
            harm_counts,
            freq_index,
            blade_counts,
        )
        results = [pltpu.with_memory_space_constraint(r, pltpu.VMEM) for r in results]
        return pl.pallas_call(
            write_kernel,
            name="write",
            out_shape=tuple(jax.ShapeDtypeStruct(o.shape, f32) for o in outs),
            in_specs=[vmem, vmem, vmem],
            out_specs=[any_spec, any_spec, any_spec],
            scratch_shapes=[dma((3,))],
        )(*results)

    in_specs = (P(("blk", "harm"), None), P(None, "harm", "blk", None), P(), P("blk"), P(), P(), P())
    out_specs = (P(None, "harm", "blk", None), P(("blk", "harm"), None), P(("blk", "harm"), None))
    return jax.shard_map(shards, mesh=mesh, in_specs=in_specs, out_specs=out_specs, check_vma=False)
```

```python
import functools

import jax
import jax.numpy as jnp
from jax import lax
from jax.experimental import pallas as pl
from jax.experimental.pallas import tpu as pltpu
from jax.sharding import PartitionSpec as P

MESH = pl.DeviceIdType.MESH
relax_rate = 0.3
LANES = 128
SUB = 8


HOPS = (4, 3, 5, 2, 6, 1, 7, 0)


def fourier_kernel(
    n_blk,
    n_harm,
    samples_hbm,
    store_hbm,
    phase_hbm,
    patch_row_hbm,
    harm_counts_hbm,
    freq_index_hbm,
    blade_counts_hbm,
    new_store,
    lower,
    upper,
    store,
    gathered,
    freq,
    rows,
    coef,
    mine,
    theirs,
    inbox,
    outbox,
    passing,
    arrived,
    phase,
    harm_counts,
    blade_counts,
    patch_row,
    freq_index,
    around,
    beyond,
    small_sem,
    own_sem,
    load_sem,
    pair_send,
    pair_recv,
    pass_send,
    pass_recv,
    sum_send,
    sum_recv,
    ring_send,
    ring_recv,
    fwd_send,
    fwd_recv,
):
    slots, patches = store.shape[1], store.shape[2]
    row_count, slot_total = freq_index.shape
    ring = n_harm // 2
    share = patches // n_harm
    tiles = share // SUB
    blk = lax.axis_index("blk")
    harm = lax.axis_index("harm")
    chip, core = harm // 2, harm % 2
    partner = 2 * chip + 1 - core
    after = lax.rem(blk + 1, n_blk)
    before = lax.rem(blk + n_blk - 1, n_blk)

    def signal(sem, b, h):
        pl.semaphore_signal(sem, 1, device_id=(b, h), device_id_type=MESH)

    def remote(src, dst, send, recv, device):
        return pltpu.make_async_remote_copy(
            src_ref=src, dst_ref=dst, send_sem=send, recv_sem=recv, device_id=device, device_id_type=MESH
        )

    def peer(d):
        return 2 * lax.rem(chip + d, ring) + core

    def peer(d):
        return 2 * lax.rem(chip + d, ring) + core

    barrier = pltpu.get_barrier_semaphore()
    for d in (2, 6, 1, 7):
        signal(barrier, blk, peer(d) - core)
    signal(barrier, after, 2 * chip + 1)
    signal(barrier, before, 2 * chip + 1)

    @pl.when(core == 1)
    def _():
        signal(barrier, blk, partner)

    small = []
    for i, (src, dst) in enumerate(
        (
            (phase_hbm, phase),
            (harm_counts_hbm, harm_counts),
            (blade_counts_hbm, blade_counts),
            (freq_index_hbm, freq_index),
            (patch_row_hbm, patch_row),
        )
    ):
        small.append(pltpu.make_async_copy(src, dst, small_sem.at[i]))
        small[-1].start()

    def chip_at(k):
        return lax.rem(chip + HOPS[k], ring)

    loads = []
    for k in range(ring):
        at = pl.ds(pl.multiple_of(chip_at(k) * 2 * share, 2 * share), 2 * share)
        loads.append(pltpu.make_async_copy(store_hbm.at[:, :, at], store.at[:, :, at], load_sem.at[k]))
        if k < 3:
            loads[-1].start()
    own = pltpu.make_async_copy(samples_hbm, gathered.at[harm], own_sem)
    own.start()

    for copy in small:
        copy.wait()
    for k in range(3, ring):
        loads[k].start()
    sub = lax.broadcasted_iota(jnp.int32, (SUB, LANES), 0)
    lane = lax.broadcasted_iota(jnp.int32, (SUB, LANES), 1)
    freq[...] = jnp.zeros((SUB, LANES), jnp.float32)
    freq[:row_count, :slot_total] = freq_index[...].astype(jnp.float32)
    frequency = freq[...]

    def by_row(ref, other):
        out = jnp.full((SUB, LANES), other)
        for r in range(row_count):
            out = jnp.where(sub == r, ref[r], out)
        return out

    now = frequency * by_row(phase, jnp.float32(0))
    blades = by_row(blade_counts, jnp.int32(1)).astype(jnp.float32)
    lag = 2.0 * jnp.pi * frequency / blades
    active = lane < by_row(harm_counts, jnp.int32(0))
    now_cos, now_sin = jnp.cos(now), jnp.sin(now)
    back, ahead = now - lag, now + lag
    back_cos, back_sin = jnp.cos(back), jnp.sin(back)
    ahead_cos, ahead_sin = jnp.cos(ahead), jnp.sin(ahead)
    gain = 2.0 * relax_rate
    keep = 1.0 - relax_rate
    zero = jnp.zeros((SUB, LANES), jnp.float32)

    def spread(table):
        return jnp.broadcast_to(jnp.sum(table, axis=1, keepdims=True), (SUB, LANES))

    for j in range(slots):
        here = lane == harm * slots + j
        on = active & here
        for i, table in enumerate((back_cos, back_sin, ahead_cos, ahead_sin)):
            coef[j, i] = spread(jnp.where(on, keep * table, zero))
        coef[j, 4] = spread(jnp.where(on, gain * now_cos, zero))
        coef[j, 5] = spread(jnp.where(on, gain * now_sin, zero))
        coef[j, 6] = spread(jnp.where(here, jnp.where(active, keep, 1.0), zero))
    back_gain = spread(jnp.where(active, gain * (now_cos * back_cos + now_sin * back_sin), zero))
    ahead_gain = spread(jnp.where(active, gain * (now_cos * ahead_cos + now_sin * ahead_sin), zero))

    for i in range(patches // LANES):
        line = jnp.broadcast_to(patch_row[i : i + 1, :], (LANES, LANES))
        rows[pl.ds(i * LANES, LANES), :] = line.T

    def pick(table, row):
        return jnp.take_along_axis(table, row, axis=0, mode="promise_in_bounds")

    tables = [[coef[j, i] for i in range(4)] for j in range(slots)]

    def partial(base):
        row = rows[pl.ds(base, SUB), :]
        back_sum, ahead_sum = zero, zero
        for j in range(slots):
            c, s = store[0, j, pl.ds(base, SUB), :], store[1, j, pl.ds(base, SUB), :]
            back_sum += pick(tables[j][0], row) * c + pick(tables[j][1], row) * s
            ahead_sum += pick(tables[j][2], row) * c + pick(tables[j][3], row) * s
        return back_sum, ahead_sum

    def step_chip(k):
        step = jnp.where(lax.rem(k, 2) == 0, k // 2, ring - (k + 1) // 2)
        return lax.rem(chip + ring // 2 + step, ring)

    def pair_copy(k):
        return remote(theirs.at[k], inbox.at[k], pair_send, pair_recv.at[k], (blk, partner))

    def partial_step(k, carry):
        at = pl.ds(pl.multiple_of(step_chip(k) * 2 * share, 2 * share), 2 * share)
        pltpu.make_async_copy(store_hbm.at[:, :, at], store.at[:, :, at], load_sem.at[k]).wait()
        first = step_chip(k) * 2 * share
        for t in range(tiles):
            base = pl.multiple_of(first + (1 - core) * share + t * SUB, SUB)
            theirs[k, 0, pl.ds(t * SUB, SUB), :], theirs[k, 1, pl.ds(t * SUB, SUB), :] = partial(base)
        for t in range(tiles):
            base = pl.multiple_of(first + core * share + t * SUB, SUB)
            mine[k, 0, pl.ds(t * SUB, SUB), :], mine[k, 1, pl.ds(t * SUB, SUB), :] = partial(base)
        return carry

    lax.fori_loop(0, 3, partial_step, 0)

    def update(h):
        for t in range(tiles):
            at = pl.ds(pl.multiple_of(h * share + t * SUB, SUB), SUB)
            row = rows[at, :]
            value = gathered[h, pl.ds(t * SUB, SUB), :]
            for j in range(slots):
                hold = pick(coef[j, 6], row)
                new_store[0, j, at, :] = hold * store[0, j, at, :] + pick(coef[j, 4], row) * value
                new_store[1, j, at, :] = hold * store[1, j, at, :] + pick(coef[j, 5], row) * value

    @pl.when(core == 0)
    def _():
        pl.semaphore_wait(barrier, 9)
        signal(around, blk, partner)

    @pl.when(core == 1)
    def _():
        pl.semaphore_wait(around, 1)

    def place(d):
        return gathered.at[peer(d)]

    def block_to(d, recv):
        return remote(samples_hbm, place(0), ring_send, ring_recv.at[recv], (blk, peer(d)))

    def forward(slot, d):
        return remote(place(d) if d else samples_hbm, place(d), fwd_send, fwd_recv.at[slot], (blk, partner))

    for k in range(3):
        pair_copy(k).start()
    block_to(2, 2).start()
    block_to(6, 3).start()
    forward(0, 0).start()
    lax.fori_loop(3, ring, partial_step, 0)
    own.wait()
    update(harm)
    for k in range(3, ring):
        pair_copy(k).start()

    def sums_to(k):
        for i, b in enumerate((after, before)):
            source, target = outbox.at[k, i], arrived.at[k - 3, i]
            remote(source, target, sum_send, sum_recv, (b, peer(HOPS[k]))).start()

    def far(k):
        if k:
            at = pl.ds(2 * k - 2, 2)
            sem = pass_recv.at[k - 1]
            remote(outbox.at[k], passing.at[at], pass_send, sem, (blk, peer((1, 7)[k - 1]))).start()
        else:
            pass_back.start()
            pass_ahead.start()

    pass_back = remote(outbox.at[0, 0], passing.at[4], pass_send, pass_recv.at[2], (blk, peer(2)))
    pass_ahead = remote(outbox.at[0, 1], passing.at[5], pass_send, pass_recv.at[3], (blk, peer(6)))

    for k in range(3):
        pair_copy(k).wait_recv()
        outbox[k] = mine[k] + inbox[k]
        if k:
            far(k - 1)
    block_to(1, 0).start()
    block_to(7, 1).start()
    far(2)
    for k in range(3, ring - 1):
        pair_copy(k).wait_recv()
        outbox[k] = mine[k] + inbox[k]
    pair_copy(ring - 1).wait_recv()
    for t in range(tiles):
        at = pl.ds(t * SUB, SUB)
        row = rows[pl.ds(pl.multiple_of(harm * share + t * SUB, SUB), SUB), :]
        value = gathered[harm, at, :]
        k = ring - 1
        outbox[k, 0, at, :] = mine[k, 0, at, :] + inbox[k, 0, at, :] + pick(back_gain, row) * value
        outbox[k, 1, at, :] = mine[k, 1, at, :] + inbox[k, 1, at, :] + pick(ahead_gain, row) * value

    @pl.when(core == 1)
    def _():
        pl.semaphore_wait(barrier, 4)
        for b in (after, before):
            signal(beyond, b, 2 * chip)
            signal(beyond, b, 2 * chip + 1)

    top, bottom = pl.ds(0, share // 2), pl.ds(share // 2, share // 2)

    def relay(src, slot, d):
        return remote(src, src, ring_send, ring_recv.at[slot], (blk, peer(d)))

    block_to(2, 2).wait_recv()
    relay(place(6), 4, 1).start()
    relay(place(6).at[top], 6, 2).start()
    block_to(6, 3).wait_recv()
    relay(place(2), 5, 7).start()
    relay(place(2).at[bottom], 7, 6).start()
    forward(1, 6).start()
    forward(2, 2).start()

    pl.semaphore_wait(beyond, 2)
    for k in (5, 6, 7):
        sums_to(k)

    def received(ref, sem):
        pltpu.make_async_copy(ref, ref, sem).wait()

    received(passing.at[pl.ds(0, 2)], pass_recv.at[0])
    received(passing.at[4], pass_recv.at[2])
    outbox[3, 0] = outbox[3, 0] + passing[0] + passing[4]
    outbox[3, 1] = outbox[3, 1] + passing[1]
    received(passing.at[pl.ds(2, 2)], pass_recv.at[1])
    received(passing.at[5], pass_recv.at[3])
    outbox[4, 0] = outbox[4, 0] + passing[2]
    outbox[4, 1] = outbox[4, 1] + passing[3] + passing[5]
    sums_to(3)
    update(peer(6))
    sums_to(4)
    update(peer(2))
    block_to(1, 0).wait_recv()
    forward(3, 7).start()
    block_to(7, 1).wait_recv()
    forward(4, 1).start()
    update(peer(7))
    update(peer(1))

    received(place(5), ring_recv.at[4])
    forward(5, 5).start()
    received(place(3), ring_recv.at[5])
    forward(6, 3).start()
    received(place(4).at[top], ring_recv.at[6])
    received(place(4).at[bottom], ring_recv.at[7])
    forward(7, 4).start()
    for d in (5, 3, 4):
        update(peer(d))
    for slot, d in enumerate((0, 6, 2, 7, 1, 5, 3, 4)):
        h = 2 * lax.rem(chip + d, ring) + 1 - core
        received(gathered.at[h], fwd_recv.at[slot])
        update(h)

    received(arrived, sum_recv)
    for i, out in enumerate((lower, upper)):
        total = arrived[0, i]
        for k in range(1, arrived.shape[0]):
            total += arrived[k, i]
        out[...] = total
    received(theirs, pair_send)
    received(outbox.at[pl.ds(0, 3)], pass_send)
    received(arrived, sum_send)
    received(gathered.at[pl.ds(0, 7)], ring_send)
    received(gathered.at[pl.ds(0, ring)], fwd_send)


def write_kernel(a, b, c, a_out, b_out, c_out, sems):
    copies = [
        pltpu.make_async_copy(src, dst, sems.at[i])
        for i, (src, dst) in enumerate(((a, a_out), (b, b_out), (c, c_out)))
    ]
    for copy in copies:
        copy.start()
    for copy in copies:
        copy.wait()


def solution(mesh):
    n_blk, n_harm = mesh.shape["blk"], mesh.shape["harm"]
    ring = n_harm // 2

    def shards(samples, store, phase, patch_row, harm_counts, freq_index, blade_counts):
        share, points = samples.shape
        _, slots, patches, _ = store.shape
        f32 = jnp.float32
        any_spec = pl.BlockSpec(memory_space=pl.ANY)
        vmem = pl.BlockSpec(memory_space=pltpu.VMEM)
        dma = pltpu.SemaphoreType.DMA
        outs = (
            pltpu.VMEM(store.shape, f32),
            pltpu.VMEM(samples.shape, f32),
            pltpu.VMEM(samples.shape, f32),
        )
        block = (ring, 2, share, points)
        results = pl.pallas_call(
            functools.partial(fourier_kernel, n_blk, n_harm),
            name="fourier",
            out_shape=outs,
            in_specs=[any_spec] * 7,
            out_specs=[vmem, vmem, vmem],
            scratch_shapes=[
                pltpu.VMEM(store.shape, f32),
                pltpu.VMEM((n_harm, share, points), f32),
                pltpu.VMEM((SUB, LANES), f32),
                pltpu.VMEM((patches, LANES), jnp.int32),
                pltpu.VMEM((slots, 7, SUB, LANES), f32),
                pltpu.VMEM(block, f32),
                pltpu.VMEM(block, f32),
                pltpu.VMEM(block, f32),
                pltpu.VMEM(block, f32),
                pltpu.VMEM((6, share, points), f32),
                pltpu.VMEM((5, 2, share, points), f32),
                pltpu.SMEM(phase.shape, f32),
                pltpu.SMEM(harm_counts.shape, jnp.int32),
                pltpu.SMEM(blade_counts.shape, jnp.int32),
                pltpu.VMEM((patches // LANES, LANES), jnp.int32),
                pltpu.VMEM(freq_index.shape, jnp.int32),
                pltpu.SemaphoreType.REGULAR,
                pltpu.SemaphoreType.REGULAR,
                dma((5,)),
                dma(()),
                dma((ring,)),
                dma(()),
                dma((ring,)),
                dma(()),
                dma((4,)),
                dma(()),
                dma(()),
                dma(()),
                dma((8,)),
                dma(()),
                dma((ring,)),
            ],
            compiler_params=pltpu.CompilerParams(collective_id=0, has_side_effects=True),
        )(
            samples,
            store,
            phase,
            patch_row.reshape(patches // LANES, LANES),
            harm_counts,
            freq_index,
            blade_counts,
        )
        results = [pltpu.with_memory_space_constraint(r, pltpu.VMEM) for r in results]
        return pl.pallas_call(
            write_kernel,
            name="write",
            out_shape=tuple(jax.ShapeDtypeStruct(o.shape, f32) for o in outs),
            in_specs=[vmem, vmem, vmem],
            out_specs=[any_spec, any_spec, any_spec],
            scratch_shapes=[dma((3,))],
        )(*results)

    in_specs = (P(("blk", "harm"), None), P(None, "harm", "blk", None), P(), P("blk"), P(), P(), P())
    out_specs = (P(None, "harm", "blk", None), P(("blk", "harm"), None), P(("blk", "harm"), None))
    return jax.shard_map(shards, mesh=mesh, in_specs=in_specs, out_specs=out_specs, check_vma=False)
```
